32 devices in a mesh: seq: 16 (over z, y, x), head: 2 (over core).
Axes of the slice: x: 2, y: 2, z: 4, core: 2. Of those that a mesh axis runs over, the one named last changes fastest.
Arguments:
- raw_keys: bfloat16 [2, 16384, 8, 128], P(None, 'seq', 'head'), may hold values from -6 to 6
- raw_values: bfloat16 [2, 16384, 8, 128], P(None, 'seq', 'head'), may hold values from -6 to 6
- phase: int32 [2], replicated, may hold values from 0 to 255, as said below
- ratio: int32 [2, 16], replicated, may hold values from 8 to 32, as said below
- resident_len: int32 [2, 16], replicated, may hold values from 1 to 256, as said below
- beacon_queries: bfloat16 [2, 2048, 8, 8, 128], P(None, 'seq', 'head'), may hold values from -150 to 150
- beacon_wk: bfloat16 [8192, 1024], P('seq', 'head'), may hold values from -0.125 to 0.125
- beacon_wv: bfloat16 [8192, 1024], P('seq', 'head'), may hold values from -0.125 to 0.125
- resident_keys: bfloat16 [2, 4096, 8, 128], P(None, 'seq', 'head'), may hold values from -6 to 6
- resident_values: bfloat16 [2, 4096, 8, 128], P(None, 'seq', 'head'), may hold values from -6 to 6
- decode_queries: bfloat16 [4, 2, 8, 8, 128], P(None, None, 'head'), may hold values from -150 to 150
- out_weight: bfloat16 [8192, 8192], P('head', 'seq'), may hold values from -0.0625 to 0.0625
Outputs:
- beacon_keys: bfloat16 [2, 2048, 8, 128], P(None, 'seq', 'head')
- beacon_values: bfloat16 [2, 2048, 8, 128], P(None, 'seq', 'head')
- projected: bfloat16 [4, 2, 8192], P(None, None, 'seq')
The draws below stay inside these ranges and needn't reach their ends.
Inputs may be any that keep to these rules, and one draw needn't show every extreme that they name: `phase`: some request has 255. `ratio`: each value is 1024 // 128 times 1, 2 or 4; both ends occur. `resident_len`: some pair has 256.
All inputs are finite; a program needn't handle non-finite values.
Results may differ from the reference program's by a relative error of at most 0.025.
Values may be sent and summed in bfloat16 or wider, within the bound.
A program may use at most 64 MiB of HBM per device.

```python
import math
import jax
import jax.numpy as jnp
from jax import lax

KVH = 8
G = 8
HD = 128
D = 8192
INTERVAL = 1024
NB = 128
OFF = 256
REQ = 2
RES_DEV = 256
STEPS = 4
N_SEQ = 16


def draw_phase(key, part):
    base = jax.random.randint(key, (REQ,), 0, OFF)
    chosen = jax.random.randint(jax.random.fold_in(key, 7), (), 0, REQ)
    return jnp.where(jnp.arange(REQ) == chosen, OFF - 1, base).astype(jnp.int32)


def draw_ratio(key, part):
    power = jax.random.randint(key, (REQ, N_SEQ), 0, 3)
    flat_ids = jnp.arange(REQ * N_SEQ).reshape(REQ, N_SEQ)
    chosen = jax.random.randint(jax.random.fold_in(key, 3), (), 0, REQ * N_SEQ)
    power = jnp.where(flat_ids == chosen, 0, power)
    power = jnp.where(flat_ids == (chosen + 1) % (REQ * N_SEQ), 2, power)
    factor = jnp.where(power == 0, 1, jnp.where(power == 1, 2, 4))
    return (INTERVAL // NB * factor).astype(jnp.int32)


def draw_resident_len(key, part):
    base = jax.random.randint(key, (REQ, N_SEQ), 1, RES_DEV + 1)
    flat_ids = jnp.arange(REQ * N_SEQ).reshape(REQ, N_SEQ)
    chosen = jax.random.randint(jax.random.fold_in(key, 5), (), 0, REQ * N_SEQ)
    return jnp.where(flat_ids == chosen, RES_DEV, base).astype(jnp.int32)


def anchor_rows(key):
    anchors = jax.random.normal(jax.random.fold_in(key, 41), (REQ, N_SEQ, KVH, HD), jnp.float32)
    length = jnp.sqrt(jnp.sum(anchors * anchors, axis=-1, keepdims=True))
    anchors = anchors * (math.sqrt(HD) / length)
    return jnp.clip(anchors, -6.0, 6.0).astype(jnp.bfloat16).astype(jnp.float32)


def draw_resident_keys(key, part):
    whole = jax.random.normal(jax.random.fold_in(key, 42), (REQ, N_SEQ, RES_DEV, KVH, HD), jnp.float32)
    whole = jnp.clip(whole, -6.0, 6.0)
    whole = whole.at[:, :, 0].set(anchor_rows(key))
    return whole.reshape(REQ, N_SEQ * RES_DEV, KVH, HD).astype(jnp.bfloat16)


def draw_beacon_queries(key, part):
    inner = jax.random.fold_in(key, 21)
    shape = (REQ, N_SEQ * NB, KVH, G, HD)
    base = jax.random.normal(inner, shape, jnp.float32)
    return jnp.clip(2.0 * base, -12.0, 12.0).astype(jnp.bfloat16)


def draw_decode_queries(key, part):
    inner = jax.random.fold_in(key, 22)
    shape = (STEPS, REQ, KVH, G, HD)
    base = jax.random.normal(inner, shape, jnp.float32)
    return jnp.clip(2.5 * base, -12.0, 12.0).astype(jnp.bfloat16)


def steps_of(own_key, shape, split, smallest, high):
    level, own = 1.0, jax.random.fold_in(own_key, 6)
    for axis_at, shards_of in split:
        draws = jnp.exp(jax.random.uniform(jax.random.fold_in(own, axis_at), (shards_of,), jnp.float32, smallest / len(split), high / len(split)))
        level = level * jnp.repeat(draws, shape[axis_at] // shards_of).reshape([-1 if axis == axis_at else 1 for axis in range(len(shape))])
    return level


def noise(own_key, shape, spread, bound, pieces=(), kind=jnp.bfloat16):
    array = spread * jax.random.normal(own_key, shape, jnp.float32)
    if pieces:
        array = array * steps_of(own_key, shape, pieces, -0.22, 0.18)
    return jnp.clip(array, -bound, bound).astype(kind)


def setup_inputs(seed: int = 0) -> dict:
    key_list = jax.random.split(jax.random.key(seed), 13)
    raw_keys = noise(key_list[0], (REQ, INTERVAL * N_SEQ, KVH, HD), 1.0, 6.0, ((1, 16), (2, 2)))
    raw_values = noise(key_list[1], (REQ, INTERVAL * N_SEQ, KVH, HD), 1.0, 6.0, ((1, 16), (2, 2)))
    phase = draw_phase(jax.random.fold_in(key_list[12], 71), 0)
    ratio = draw_ratio(jax.random.fold_in(key_list[12], 71), 0)
    resident_len = draw_resident_len(jax.random.fold_in(key_list[12], 71), 0)
    beacon_queries = draw_beacon_queries(jax.random.fold_in(key_list[12], 71), 0)
    beacon_wk = noise(key_list[6], (D, KVH * HD), (D // 4) ** -0.5, 0.125, ((0, 16), (1, 2)))
    beacon_wv = noise(key_list[7], (D, KVH * HD), (D // 4) ** -0.5, 0.125, ((0, 16), (1, 2)))
    resident_keys = draw_resident_keys(jax.random.fold_in(key_list[12], 71), 0)
    resident_values = noise(key_list[9], (REQ, N_SEQ * RES_DEV, KVH, HD), 1.0, 6.0, ((1, 16), (2, 2)))
    decode_queries = draw_decode_queries(jax.random.fold_in(key_list[12], 71), 0)
    out_weight = noise(key_list[11], (D, D), D ** -0.5, 0.0625, ((0, 2), (1, 16)))
    return dict(raw_keys=raw_keys, raw_values=raw_values, phase=phase, ratio=ratio, resident_len=resident_len, beacon_queries=beacon_queries, beacon_wk=beacon_wk, beacon_wv=beacon_wv, resident_keys=resident_keys, resident_values=resident_values, decode_queries=decode_queries, out_weight=out_weight)


masked_score = -1e+30

def reference(raw_keys, raw_values, phase, ratio, resident_len, beacon_queries, beacon_wk, beacon_wv, resident_keys, resident_values, decode_queries, out_weight):
    requests = raw_keys.shape[0]
    heads = raw_keys.shape[2]
    inv_root = 1.0 / math.sqrt(HD)
    shaped_keys = raw_keys.reshape(requests, N_SEQ, INTERVAL, heads, HD)
    shaped_values = raw_values.reshape(requests, N_SEQ, INTERVAL, heads, HD)
    tails_k = shaped_keys[:, :, INTERVAL - OFF:]
    tails_v = shaped_values[:, :, INTERVAL - OFF:]
    near_keys = jnp.concatenate([jnp.zeros_like(tails_k[:, :1]), tails_k[:, :-1]], axis=1)
    near_values = jnp.concatenate([jnp.zeros_like(tails_v[:, :1]), tails_v[:, :-1]], axis=1)
    window_keys = jnp.moveaxis(jnp.concatenate([near_keys, shaped_keys], axis=2), 1, 0)
    window_values = jnp.moveaxis(jnp.concatenate([near_values, shaped_values], axis=2), 1, 0)
    queries = jnp.moveaxis(beacon_queries.reshape(requests, N_SEQ, NB, heads, G, HD), 1, 0)
    slot_ids = jnp.arange(NB, dtype=jnp.int32)
    row_ids = jnp.arange(OFF + INTERVAL, dtype=jnp.int32)
    key_map = beacon_wk.astype(jnp.float32)
    value_map = beacon_wv.astype(jnp.float32)

    def per_shard(members):
        shard_index, query_block, key_rows, value_rows, shard_ratio = members
        positions = row_ids[None, :] - OFF + phase[:, None]
        present = (shard_index > 0) | (positions >= phase[:, None])
        lead_in = jnp.where(shard_index == 0, phase, 0)
        reaches = (slot_ids[None, :] + 1) * shard_ratio[:, None] + lead_in[:, None]
        allowed = present[:, None, :] & (positions >= 0)[:, None, :] & (positions < INTERVAL)[:, None, :] & (positions[:, None, :] < reaches[:, :, None])
        scores = jnp.einsum('rjkgd,rikd->rjkgi', query_block.astype(jnp.float32), key_rows.astype(jnp.float32)) * inv_root
        cache_mask = allowed[:, :, None, None, :]
        row_peak = lax.optimization_barrier(jnp.max(jnp.where(cache_mask, scores, masked_score), axis=-1, keepdims=True))
        weights = jnp.where(cache_mask, jnp.exp(scores - row_peak), 0.0)
        weight_sum = lax.optimization_barrier(jnp.sum(weights, axis=-1))
        rounded = lax.optimization_barrier(weights.astype(jnp.bfloat16))
        weighted = jnp.einsum('rjkgi,rikd->rjkgd', rounded.astype(jnp.float32), value_rows.astype(jnp.float32))
        pooled = lax.optimization_barrier((weighted / weight_sum[..., None]).astype(jnp.bfloat16))
        pooled_flat = pooled.reshape(requests, NB, heads * G * HD).astype(jnp.float32)
        made_keys = jnp.einsum('rjx,xy->rjy', pooled_flat, key_map).reshape(requests, NB, heads, HD)
        made_values = jnp.einsum('rjx,xy->rjy', pooled_flat, value_map).reshape(requests, NB, heads, HD)
        slot_live = (slot_ids[None, :] < (INTERVAL // shard_ratio)[:, None])[:, :, None, None]
        return (jnp.where(slot_live, made_keys, 0.0).astype(jnp.bfloat16), jnp.where(slot_live, made_values, 0.0).astype(jnp.bfloat16))
    made_k, made_v = lax.map(per_shard, (jnp.arange(N_SEQ, dtype=jnp.int32), queries, window_keys, window_values, jnp.transpose(ratio)))
    beacon_keys = jnp.moveaxis(made_k, 0, 1).reshape(requests, N_SEQ * NB, heads, HD)
    beacon_values = jnp.moveaxis(made_v, 0, 1).reshape(requests, N_SEQ * NB, heads, HD)
    leftover_keys = shaped_keys[:, N_SEQ - 1, INTERVAL - OFF:]
    leftover_values = shaped_values[:, N_SEQ - 1, INTERVAL - OFF:]
    cache_keys = jnp.concatenate([resident_keys, beacon_keys, leftover_keys], axis=1)
    cache_values = jnp.concatenate([resident_values, beacon_values, leftover_values], axis=1)
    resident_ok = (jnp.arange(RES_DEV, dtype=jnp.int32)[None, None, :] < resident_len[:, :, None]).reshape(requests, N_SEQ * RES_DEV)
    beacon_ok = (slot_ids[None, None, :] < (INTERVAL // ratio)[:, :, None]).reshape(requests, N_SEQ * NB)
    leftover_ok = jnp.arange(OFF, dtype=jnp.int32)[None, :] >= OFF - phase[:, None]
    usable = jnp.concatenate([resident_ok, beacon_ok, leftover_ok], axis=1)
    scores = jnp.einsum('srkgd,rikd->rksgi', decode_queries.astype(jnp.float32), cache_keys.astype(jnp.float32)) * inv_root
    cache_mask = usable[:, None, None, None, :]
    row_peak = lax.optimization_barrier(jnp.max(jnp.where(cache_mask, scores, masked_score), axis=-1, keepdims=True))
    weights = jnp.where(cache_mask, jnp.exp(scores - row_peak), 0.0)
    weight_sum = lax.optimization_barrier(jnp.sum(weights, axis=-1))
    rounded = lax.optimization_barrier(weights.astype(jnp.bfloat16))
    weighted = jnp.einsum('rksgi,rikd->rksgd', rounded.astype(jnp.float32), cache_values.astype(jnp.float32))
    attended = (weighted / weight_sum[..., None]).astype(jnp.bfloat16)
    attended = jnp.transpose(attended, (2, 0, 1, 3, 4)).reshape(STEPS * requests, D)
    projected = jnp.dot(attended, out_weight, preferred_element_type=jnp.float32).astype(jnp.bfloat16)
    return (beacon_keys, beacon_values, projected.reshape(STEPS, requests, D))
```

```python
import functools
import math

import jax
import jax.numpy as jnp
from jax import lax
from jax.experimental import pallas as pl
from jax.experimental.pallas import tpu as pltpu
from jax.sharding import PartitionSpec as P

G = 8
INTERVAL = 1024
NB = 128
OFF = 256
STEPS = 4


masked_score = -1e30


def shifted(value, axis, steps):
    count = lax.axis_size(axis)
    first, last = (max(0, -steps), min(count, count - steps))
    return lax.ppermute(value, axis, [(source, source + steps) for source in range(first, last)])


def joined(shard, axis, combine):
    everything = jax.tree.map(lambda part: lax.all_gather(part, axis), shard)
    first = jax.tree.map(lambda part: part[0], everything)

    def hop(k, so_far):
        return combine(so_far, jax.tree.map(lambda part: part[k], everything))

    return lax.fori_loop(1, lax.axis_size(axis), hop, first)


def blend(former, latter):
    row_peak = jnp.maximum(former[0], latter[0])
    former_scale = jnp.exp(former[0] - row_peak)
    latter_scale = jnp.exp(latter[0] - row_peak)
    weight_sum = former[1] * former_scale + latter[1] * latter_scale
    weighted = former[2] * former_scale[..., None] + latter[2] * latter_scale[..., None]
    return (row_peak, weight_sum, weighted)


def pool_part(queries, key_rows, value_rows, positions, present, reaches):
    inv_root = 1.0 / math.sqrt(queries.shape[-1])

    def per_request(members):
        query_block, key_block, value_block, position_row, present_row, reach_row = members
        scores = (
            jnp.einsum("jkgd,ikd->jkgi", query_block, key_block, preferred_element_type=jnp.float32)
            * inv_root
        )
        allowed = (
            present_row[None, :]
            & (position_row[None, :] >= 0)
            & (position_row[None, :] < INTERVAL)
            & (position_row[None, :] < reach_row[:, None])
        )
        cache_mask = allowed[:, None, None, :]
        row_peak = jnp.max(jnp.where(cache_mask, scores, masked_score), axis=-1)
        weights = jnp.where(cache_mask, jnp.exp(scores - row_peak[..., None]), 0.0)
        weight_sum = jnp.sum(weights, axis=-1)
        weighted = jnp.einsum(
            "jkgi,ikd->jkgd",
            weights.astype(jnp.bfloat16),
            value_block,
            preferred_element_type=jnp.float32,
        )
        return (row_peak, weight_sum, weighted)

    return lax.map(per_request, (queries, key_rows, value_rows, positions, present, reaches))


def body(
    raw_keys,
    raw_values,
    phase,
    ratio,
    resident_len,
    beacon_queries,
    beacon_wk,
    beacon_wv,
    resident_keys,
    resident_values,
    decode_queries,
    out_weight,
):
    requests = raw_keys.shape[0]
    kv_local = raw_keys.shape[2]
    head_dim = raw_keys.shape[3]
    shard_index = lax.axis_index("seq")
    shard_count = lax.axis_size("seq")
    is_first = shard_index == 0
    is_last = shard_index == shard_count - 1
    own_ratio = lax.dynamic_index_in_dim(ratio, shard_index, 1, keepdims=False)
    slot_ids = jnp.arange(NB, dtype=jnp.int32)
    lead_in = jnp.where(is_first, phase, 0)
    reaches = (slot_ids[None, :] + 1) * own_ratio[:, None] + lead_in[:, None]
    tail_keys = raw_keys[:, INTERVAL - OFF :]
    tail_values = raw_values[:, INTERVAL - OFF :]
    own_positions = jnp.arange(INTERVAL, dtype=jnp.int32)[None, :] + phase[:, None]
    rim_ids = jnp.arange(OFF, dtype=jnp.int32)
    rim_positions = rim_ids[None, :] - OFF + phase[:, None]
    near_keys, near_values = shifted((tail_keys, tail_values), "seq", 1)
    key_rows = jnp.concatenate([near_keys, raw_keys], axis=1)
    value_rows = jnp.concatenate([near_values, raw_values], axis=1)
    positions = jnp.concatenate([rim_positions, own_positions], axis=1)
    present = jnp.logical_not(is_first) | (positions >= phase[:, None])
    pooled_parts = pool_part(beacon_queries, key_rows, value_rows, positions, present, reaches)
    pooled = (pooled_parts[2] / pooled_parts[1][..., None]).astype(jnp.bfloat16)
    pooled_flat = pooled.reshape(requests * NB, kv_local * G * head_dim)
    pooled_whole = lax.all_gather(pooled_flat, "head", axis=1, tiled=True)
    key_sum = jnp.dot(
        pooled_whole,
        lax.all_gather(beacon_wk, "seq", axis=0, tiled=True),
        preferred_element_type=jnp.float32,
    )
    value_sum = jnp.dot(
        pooled_whole,
        lax.all_gather(beacon_wv, "seq", axis=0, tiled=True),
        preferred_element_type=jnp.float32,
    )
    made_keys = key_sum
    made_values = value_sum
    made_keys = made_keys.reshape(requests, NB, kv_local, head_dim)
    made_values = made_values.reshape(requests, NB, kv_local, head_dim)
    slot_live = slot_ids[None, :] < (INTERVAL // own_ratio)[:, None]
    beacon_keys = jnp.where(slot_live[:, :, None, None], made_keys, 0.0).astype(jnp.bfloat16)
    beacon_values = jnp.where(slot_live[:, :, None, None], made_values, 0.0).astype(jnp.bfloat16)
    cache_keys = jnp.concatenate([resident_keys, beacon_keys, tail_keys], axis=1)
    cache_values = jnp.concatenate([resident_values, beacon_values, tail_values], axis=1)
    own_len = lax.dynamic_index_in_dim(resident_len, shard_index, 1, keepdims=False)
    resident_ok = jnp.arange(resident_keys.shape[1], dtype=jnp.int32)[None, :] < own_len[:, None]
    leftover_ok = (rim_ids[None, :] >= OFF - phase[:, None]) & is_last
    usable = jnp.concatenate([resident_ok, slot_live, leftover_ok], axis=1)
    inv_root = 1.0 / math.sqrt(head_dim)
    scores = (
        jnp.einsum(
            "srkgd,rikd->rksgi", decode_queries, cache_keys, preferred_element_type=jnp.float32
        )
        * inv_root
    )
    cache_mask = usable[:, None, None, None, :]
    row_peak = jnp.max(jnp.where(cache_mask, scores, masked_score), axis=-1)
    weights = jnp.where(cache_mask, jnp.exp(scores - row_peak[..., None]), 0.0)
    weight_sum = jnp.sum(weights, axis=-1)
    weighted = jnp.einsum(
        "rksgi,rikd->rksgd",
        weights.astype(jnp.bfloat16),
        cache_values,
        preferred_element_type=jnp.float32,
    )
    merged = joined((row_peak, weight_sum, weighted), "seq", blend)
    total_sum = merged[1]
    total_weighted = merged[2]
    attended = (total_weighted / total_sum[..., None]).astype(jnp.bfloat16)
    attended = jnp.transpose(attended, (2, 0, 1, 3, 4)).reshape(
        STEPS * requests, kv_local * G * head_dim
    )
    partial_value = jnp.dot(attended, out_weight, preferred_element_type=jnp.float32)
    summed = lax.psum(partial_value, "head")
    projected = summed.astype(jnp.bfloat16).reshape(STEPS, requests, out_weight.shape[1])
    return (beacon_keys, beacon_values, projected)


B = 4
CH = 4


def fused_kernel(
    shard_count,
    phase_ref,
    ratio_ref,
    rlen_ref,
    k_hbm,
    v_hbm,
    q_hbm,
    wk_hbm,
    wv_hbm,
    rk_ref,
    rv_ref,
    dq_ref,
    ow_hbm,
    bk_ref,
    bv_ref,
    proj_ref,
    kbuf,
    vbuf,
    qbuf,
    wbuf,
    act,
    stage,
    psend,
    precv,
    own,
    bias,
    owbuf,
    snd,
    rcv,
    att,
    part,
    load_sem,
    rim_send,
    rim_recv,
    w_send,
    w_recv,
    a_send,
    a_recv,
    a_loc,
    p_send,
    p_recv,
    s_send,
    s_recv,
    d_send,
    d_recv,
    t_send,
    t_recv,
    h_send,
    h_recv,
):
    n = shard_count
    depth = n // B
    s = lax.axis_index("seq")
    h = lax.axis_index("head")
    z = s // B
    me = lax.rem(s, B)
    heads, rows, hd = kbuf.shape[1], kbuf.shape[2], kbuf.shape[3]
    requests = kbuf.shape[0]
    interval = rows - OFF
    nb = bias.shape[1]
    width = wbuf.shape[3]
    inv_root = 1.0 / math.sqrt(hd)
    f32 = jnp.float32

    def remote(src, dst, send, recv, seq=None):
        target = {"head": 1 - h} if seq is None else {"seq": seq}
        return pltpu.make_async_remote_copy(
            src_ref=src,
            dst_ref=dst,
            send_sem=send,
            recv_sem=recv,
            device_id=target,
            device_id_type=pl.DeviceIdType.MESH,
        )

    loads = []
    half = wk_hbm.shape[1] // (CH // 2)
    for c in range(CH):
        source = (wk_hbm, wv_hbm)[c // (CH // 2)]
        first = (c % (CH // 2)) * half
        loads.append(
            pltpu.make_async_copy(
                source.at[:, first : first + half], wbuf.at[z, c], load_sem.at[c]
            )
        )
    loads.append(pltpu.make_async_copy(k_hbm, kbuf.at[:, :, OFF:], load_sem.at[CH]))
    loads.append(pltpu.make_async_copy(v_hbm, vbuf.at[:, :, OFF:], load_sem.at[CH + 1]))
    loads.append(pltpu.make_async_copy(q_hbm, qbuf, load_sem.at[CH + 2]))
    loads.append(pltpu.make_async_copy(ow_hbm, owbuf, load_sem.at[CH + 3]))
    for copy in loads:
        copy.start()

    barrier = pltpu.get_barrier_semaphore()
    for o in range(1, n):
        pl.semaphore_signal(
            barrier, inc=1, device_id={"seq": lax.rem(s + o, n)}, device_id_type=pl.DeviceIdType.MESH
        )
    pl.semaphore_signal(
        barrier, inc=1, device_id={"head": 1 - h}, device_id_type=pl.DeviceIdType.MESH
    )
    pl.semaphore_wait(barrier, n)

    def rim(which):
        source, target = ((k_hbm, kbuf), (v_hbm, vbuf))[which]
        return remote(
            source.at[:, :, interval - OFF :],
            target.at[:, :, :OFF],
            rim_send.at[which],
            rim_recv.at[which],
            lax.rem(s + 1, n),
        )

    @pl.when(s < n - 1)
    def _():
        rim(0).start()
        rim(1).start()

    @pl.when(s == 0)
    def _():
        kbuf[:, :, :OFF] = jnp.zeros((requests, heads, OFF, hd), kbuf.dtype)
        vbuf[:, :, :OFF] = jnp.zeros((requests, heads, OFF, hd), vbuf.dtype)

    def w_copy(way, d, c, shard, target):
        return remote(
            wbuf.at[shard, c],
            wbuf.at[shard, c],
            w_send.at[way, d, c],
            w_recv.at[way, d, c],
            target * B + me,
        )

    def w_out(way, d):
        if way == 0:
            return z - d, z + 1, (z - d >= 0) & (z + 1 < depth)
        return z + d, z - 1, (z + d < depth) & (z - 1 >= 0)

    def w_in(way, d):
        if way == 0:
            return z - 1 - d, z - 1 - d >= 0
        return z + 1 + d, z + 1 + d < depth

    def w_start(d, c):
        for way in range(2):
            shard, target, there = w_out(way, d)

            @pl.when(there)
            def _(way=way, shard=shard, target=target):
                w_copy(way, d, c, shard, target).start()

    def w_wait(d, c):
        for way in range(2):
            shard, there = w_in(way, d)

            @pl.when(there)
            def _(way=way, shard=shard):
                w_copy(way, d, c, shard, z).wait_recv()

    def w_relay(d, c):
        for way in range(2):
            shard, there = w_in(way, d - 1)
            out, target, onward = w_out(way, d)

            @pl.when(there)
            def _(way=way, shard=shard):
                w_copy(way, d - 1, c, shard, z).wait_recv()

            @pl.when(onward)
            def _(way=way, out=out, target=target):
                w_copy(way, d, c, out, target).start()

    def w_own(c):
        loads[c].wait()
        w_start(0, c)

    w_own(0)
    w_own(1)

    for r in range(requests):
        slot = lax.broadcasted_iota(jnp.int32, (nb, rows), 0)
        position = lax.broadcasted_iota(jnp.int32, (nb, rows), 1) - OFF + phase_ref[r]
        lead = jnp.where(s == 0, phase_ref[r], 0)
        reach = (slot + 1) * ratio_ref[r, s] + lead
        allowed = (position >= lead) & (position < interval) & (position < reach)
        bias[r] = jnp.where(allowed, 0.0, masked_score).astype(f32)

    loads[CH].wait()
    loads[CH + 1].wait()
    loads[CH + 2].wait()

    w_relay(1, 0)
    w_own(2)
    w_relay(2, 0)
    w_relay(1, 1)
    w_own(3)

    @pl.when(s > 0)
    def _():
        rim(0).wait_recv()
        rim(1).wait_recv()

    def a_remote(u, x):
        kk, r, y = u // 4, lax.rem(u, 2), lax.rem(u // 2, 2)
        return remote(
            stage.at[u, x],
            act.at[h * 2 + kk, me, r],
            a_send.at[u, x],
            a_recv.at[kk, r, me],
            z * B + y * 2 + x,
        )

    def a_local(kk, r, u):
        return pltpu.make_async_copy(
            stage.at[u, lax.rem(me, 2)], act.at[h * 2 + kk, me, r], a_loc.at[kk, r]
        )

    def a_relay(kk):
        return remote(
            act.at[h * 2 + kk], act.at[h * 2 + kk], p_send.at[kk], p_recv.at[kk]
        )

    def a_gather(kk):
        for r in range(requests):
            a_local(kk, r, kk * 4 + (me // 2) * 2 + r).wait()
            for o in range(1, B):
                source = lax.rem(me + o, B)
                remote(
                    stage.at[0, 0],
                    act.at[h * 2 + kk, source, r],
                    a_send.at[0, 0],
                    a_recv.at[kk, r, source],
                    s,
                ).wait_recv()
        a_relay(kk).start()

    def unit(u, carry):
        k, r = u // 2, lax.rem(u, 2)
        for g in range(G):
            scores = (
                lax.dot_general(
                    qbuf[r, k, g],
                    kbuf[r, k],
                    (((1,), (1,)), ((), ())),
                    preferred_element_type=f32,
                )
                * inv_root
                + bias[r]
            )
            weights = jnp.exp(scores - jnp.max(scores, axis=-1, keepdims=True))
            total = jnp.sum(weights, axis=-1, keepdims=True)
            out = jnp.dot(weights.astype(jnp.bfloat16), vbuf[r, k], preferred_element_type=f32)
            at = (g % 4) * hd
            stage[u, g // 4, :, at : at + hd] = (out / total).astype(jnp.bfloat16)
        for x in range(2):
            member = lax.rem(k, 2) * 2 + x

            @pl.when(member == me)
            def _():
                a_local(u // 4, r, u).start()

            @pl.when(member != me)
            def _(x=x):
                a_remote(u, x).start()

        @pl.when(u == 1)
        def _():
            w_relay(2, 1)
            w_relay(1, 2)

        @pl.when(u == 3)
        def _():
            w_relay(2, 2)

        @pl.when(u == 5)
        def _():
            a_gather(0)
            w_relay(1, 3)

        return carry

    lax.fori_loop(0, 2 * heads, unit, 0)
    a_gather(1)
    w_relay(2, 3)
    a_relay(0).wait_recv()
    a_relay(1).wait_recv()

    def p_copy(c, to, frm):
        return remote(
            psend.at[to, c], precv.at[frm, c], s_send.at[to, c], s_recv.at[frm, c], z * B + to
        )

    for c in range(CH):
        w_wait(depth - 2, c)

        def product(o, carry, c=c):
            to = lax.rem(me + 1 + o, B)
            total = jnp.zeros((requests * nb, width), f32)
            for zi in range(depth):
                total += jnp.dot(
                    act[zi, to].reshape(requests * nb, act.shape[4]),
                    wbuf[zi, c],
                    preferred_element_type=f32,
                )

            @pl.when(o < B - 1)
            def _():
                psend[to, c] = total.astype(jnp.bfloat16)
                p_copy(c, to, me).start()

            @pl.when(o == B - 1)
            def _():
                own[c] = total

            return carry

        lax.fori_loop(0, B, product, 0)

    slot_row = lax.broadcasted_iota(jnp.int32, (nb, width), 0)
    for c in range(CH):
        for o in range(1, B):
            source = lax.rem(me + o, B)
            p_copy(c, source, source).wait_recv()
        total = own[c]
        for o in range(1, B):
            total += precv[lax.rem(me + o, B), c].astype(f32)
        out_ref = (bk_ref, bv_ref)[c // (CH // 2)]
        at = (c % (CH // 2)) * width
        for r in range(requests):
            live = (slot_row + 1) * ratio_ref[r, s] <= interval
            out_ref[r * nb : (r + 1) * nb, at : at + width] = jnp.where(
                live, total[r * nb : (r + 1) * nb], 0.0
            ).astype(jnp.bfloat16)

    res = rk_ref.shape[2]
    qrows = dq_ref.shape[1]
    pair = qrows // G
    cells = res + nb + OFF
    row_request = lax.rem(lax.broadcasted_iota(jnp.int32, (qrows, cells), 0), pair) // (
        pair // requests
    )
    cell = lax.broadcasted_iota(jnp.int32, (qrows, cells), 1)
    last = jnp.where(s == n - 1, 1, 0)
    masks = []
    for r in range(requests):
        usable = (
            (cell < rlen_ref[r, s])
            | ((cell >= res) & (cell < res + nb) & ((cell - res + 1) * ratio_ref[r, s] <= interval))
            | ((cell >= res + nb + OFF - phase_ref[r] * last) & (cell >= res + nb))
        )
        masks.append(usable & (row_request == r))
    share = G * heads // n
    for k in range(heads):
        lanes = slice(k * hd, (k + 1) * hd)
        pieces = []
        for r in range(requests):
            keys = (rk_ref[r, k], bk_ref[r * nb : (r + 1) * nb, lanes], kbuf[r, k, rows - OFF :])
            scores = jnp.concatenate(
                [
                    lax.dot_general(
                        dq_ref[k], key, (((1,), (1,)), ((), ())), preferred_element_type=f32
                    )
                    for key in keys
                ],
                axis=1,
            )
            pieces.append(jnp.where(masks[r], scores * inv_root, masked_score))
        peak = jnp.maximum(
            jnp.max(pieces[0], axis=-1, keepdims=True), jnp.max(pieces[1], axis=-1, keepdims=True)
        )
        total = jnp.zeros((qrows, 1), f32)
        out = jnp.zeros((qrows, hd), f32)
        for r in range(requests):
            weights = jnp.exp(pieces[r] - peak)
            total += jnp.sum(weights, axis=-1, keepdims=True)
            low = weights.astype(jnp.bfloat16)
            out += jnp.dot(low[:, :res], rv_ref[r, k], preferred_element_type=f32)
            out += jnp.dot(
                low[:, res : res + nb],
                bv_ref[r * nb : (r + 1) * nb, lanes],
                preferred_element_type=f32,
            )
            out += jnp.dot(
                low[:, res + nb :], vbuf[r, k, rows - OFF :], preferred_element_type=f32
            )
        lane = lax.broadcasted_iota(jnp.int32, (qrows, hd), 1)
        stats = jnp.where(lane < hd // 2, peak, total)
        snd[k * G : (k + 1) * G, 0] = out.reshape(G, pair, hd)
        snd[k * G : (k + 1) * G, 1] = stats.reshape(G, pair, hd)

    def d_copy(to, frm):
        return remote(
            snd.at[pl.ds(to * share, share)], rcv.at[frm], d_send.at[to], d_recv.at[frm], to
        )

    def t_copy(to, frm):
        return remote(att.at[frm], att.at[frm], t_send.at[to], t_recv.at[frm], to)

    for o in range(1, n):
        d_copy(lax.rem(s + o, n), s).start()
    rcv[s] = snd[pl.ds(s * share, share)]
    for o in range(1, n):
        source = lax.rem(s + o, n)
        d_copy(source, source).wait_recv()
    peaks = rcv[:, :, 1, :, 0:1]
    sums = rcv[:, :, 1, :, hd // 2 : hd // 2 + 1]
    scale = jnp.exp(peaks - jnp.max(peaks, axis=0, keepdims=True))
    att[s] = jnp.sum(scale * rcv[:, :, 0], axis=0) / jnp.sum(scale * sums, axis=0)
    for o in range(1, n):
        t_copy(lax.rem(s + o, n), s).start()
    for o in range(1, n):
        source = lax.rem(s + o, n)
        t_copy(source, source).wait_recv()
    loads[CH + 3].wait()
    vectors = jnp.concatenate(
        [att[i, j].astype(jnp.bfloat16) for i in range(n) for j in range(share)], axis=1
    )
    partial_value = jnp.dot(vectors, owbuf[...], preferred_element_type=f32)
    part[0] = partial_value
    swap = remote(part.at[0], part.at[1], h_send, h_recv)
    swap.start()
    swap.wait_recv()
    first = jnp.where(h == 0, part[0], part[1])
    second = jnp.where(h == 0, part[1], part[0])
    proj_ref[...] = (first + second).astype(jnp.bfloat16)

    swap.wait_send()
    for o in range(1, n):
        d_copy(lax.rem(s + o, n), s).wait_send()
        t_copy(lax.rem(s + o, n), s).wait_send()
    for c in range(CH):
        for o in range(1, B):
            p_copy(c, lax.rem(me + o, B), me).wait_send()
    a_relay(0).wait_send()
    a_relay(1).wait_send()
    for u in range(2 * heads):
        for x in range(2):

            @pl.when((u // 2 % 2) * 2 + x != me)
            def _(u=u, x=x):
                a_remote(jnp.int32(u), x).wait_send()

    for way in range(2):
        for d in range(depth - 1):
            shard, target, there = w_out(way, d)
            for c in range(CH):

                @pl.when(there)
                def _(way=way, d=d, c=c, shard=shard, target=target):
                    w_copy(way, d, c, shard, target).wait_send()

    @pl.when(s < n - 1)
    def _():
        rim(0).wait_send()
        rim(1).wait_send()


def fused_body(
    shard_count,
    raw_keys,
    raw_values,
    phase,
    ratio,
    resident_len,
    beacon_queries,
    beacon_wk,
    beacon_wv,
    resident_keys,
    resident_values,
    decode_queries,
    out_weight,
):
    n = shard_count
    depth = n // B
    requests, interval, heads, hd = raw_keys.shape
    steps = decode_queries.shape[0]
    nb = beacon_queries.shape[1]
    rows = interval + OFF
    by_head = (0, 2, 1, 3)
    feature, columns = beacon_wk.shape
    width = 2 * columns // CH
    pair = requests * steps
    share = G * heads // n
    bf16, f32 = jnp.bfloat16, jnp.float32
    dma = pltpu.SemaphoreType.DMA
    smem = pl.BlockSpec(memory_space=pltpu.SMEM)
    anywhere = pl.BlockSpec(memory_space=pl.ANY)
    vmem = pl.BlockSpec(memory_space=pltpu.VMEM)
    keys, values, projected = pl.pallas_call(
        functools.partial(fused_kernel, n),
        out_shape=(
            jax.ShapeDtypeStruct((requests * nb, columns), bf16),
            jax.ShapeDtypeStruct((requests * nb, columns), bf16),
            jax.ShapeDtypeStruct((pair, out_weight.shape[1]), bf16),
        ),
        in_specs=[smem] * 3 + [anywhere] * 5 + [vmem] * 3 + [anywhere],
        out_specs=(vmem, vmem, vmem),
        scratch_shapes=[
            pltpu.VMEM((requests, heads, rows, hd), bf16),
            pltpu.VMEM((requests, heads, rows, hd), bf16),
            pltpu.VMEM((requests, heads, G, nb, hd), bf16),
            pltpu.VMEM((depth, CH, feature, width), bf16),
            pltpu.VMEM((depth, B, requests, nb, feature), bf16),
            pltpu.VMEM((requests * heads, 2, nb, feature), bf16),
            pltpu.VMEM((B, CH, requests * nb, width), bf16),
            pltpu.VMEM((B, CH, requests * nb, width), bf16),
            pltpu.VMEM((CH, requests * nb, width), f32),
            pltpu.VMEM((requests, nb, rows), f32),
            pltpu.VMEM(out_weight.shape, bf16),
            pltpu.VMEM((G * heads, 2, pair, hd), f32),
            pltpu.VMEM((n, share, 2, pair, hd), f32),
            pltpu.VMEM((n, share, pair, hd), f32),
            pltpu.VMEM((2, pair, out_weight.shape[1]), f32),
            dma((CH + 4,)),
            dma((2,)),
            dma((2,)),
            dma((2, depth - 1, CH)),
            dma((2, depth - 1, CH)),
            dma((requests * heads, 2)),
            dma((2, requests, B)),
            dma((2, requests)),
            dma((2,)),
            dma((2,)),
            dma((B, CH)),
            dma((B, CH)),
            dma((n,)),
            dma((n,)),
            dma((n,)),
            dma((n,)),
            dma,
            dma,
        ],
        compiler_params=pltpu.CompilerParams(
            collective_id=0, has_side_effects=True, vmem_limit_bytes=60 * 1024 * 1024
        ),
    )(
        phase,
        ratio,
        resident_len,
        jnp.transpose(raw_keys, by_head),
        jnp.transpose(raw_values, by_head),
        jnp.transpose(beacon_queries, (0, 2, 3, 1, 4)),
        beacon_wk,
        beacon_wv,
        jnp.transpose(resident_keys, by_head),
        jnp.transpose(resident_values, by_head),
        jnp.transpose(decode_queries, (2, 3, 1, 0, 4)).reshape(heads, G * pair, hd),
        out_weight,
    )
    return (
        keys.reshape(requests, nb, heads, hd),
        values.reshape(requests, nb, heads, hd),
        jnp.transpose(projected.reshape(requests, steps, -1), (1, 0, 2)),
    )


def chosen_body(shard_count, head_count):
    def run(*arrays):
        requests, _, heads, hd = arrays[0].shape
        feature = arrays[6].shape[0]
        fits = (
            head_count == 2
            and shard_count == B * B
            and requests == 2
            and heads == B
            and 2 * feature == G * hd
        )
        return fused_body(shard_count, *arrays) if fits else body(*arrays)

    return run


def solution(mesh):
    return jax.shard_map(
        chosen_body(mesh.shape["seq"], mesh.shape["head"]),
        mesh=mesh,
        in_specs=(
            P(None, "seq", "head", None),
            P(None, "seq", "head", None),
            P(),
            P(),
            P(),
            P(None, "seq", "head", None, None),
            P("seq", "head"),
            P("seq", "head"),
            P(None, "seq", "head", None),
            P(None, "seq", "head", None),
            P(None, None, "head", None, None),
            P("head", "seq"),
        ),
        out_specs=(
            P(None, "seq", "head", None),
            P(None, "seq", "head", None),
            P(None, None, "seq"),
        ),
        check_vma=False,
    )
```

```python
import functools
import math

import jax
import jax.numpy as jnp
from jax import lax
from jax.experimental import pallas as pl
from jax.experimental.pallas import tpu as pltpu
from jax.sharding import PartitionSpec as P

G = 8
INTERVAL = 1024
NB = 128
OFF = 256
STEPS = 4


masked_score = -1e30


def shifted(value, axis, steps):
    count = lax.axis_size(axis)
    first, last = (max(0, -steps), min(count, count - steps))
    return lax.ppermute(value, axis, [(source, source + steps) for source in range(first, last)])


def joined(shard, axis, combine):
    everything = jax.tree.map(lambda part: lax.all_gather(part, axis), shard)
    first = jax.tree.map(lambda part: part[0], everything)

    def hop(k, so_far):
        return combine(so_far, jax.tree.map(lambda part: part[k], everything))

    return lax.fori_loop(1, lax.axis_size(axis), hop, first)


def blend(former, latter):
    row_peak = jnp.maximum(former[0], latter[0])
    former_scale = jnp.exp(former[0] - row_peak)
    latter_scale = jnp.exp(latter[0] - row_peak)
    weight_sum = former[1] * former_scale + latter[1] * latter_scale
    weighted = former[2] * former_scale[..., None] + latter[2] * latter_scale[..., None]
    return (row_peak, weight_sum, weighted)


def pool_part(queries, key_rows, value_rows, positions, present, reaches):
    inv_root = 1.0 / math.sqrt(queries.shape[-1])

    def per_request(members):
        query_block, key_block, value_block, position_row, present_row, reach_row = members
        scores = (
            jnp.einsum("jkgd,ikd->jkgi", query_block, key_block, preferred_element_type=jnp.float32)
            * inv_root
        )
        allowed = (
            present_row[None, :]
            & (position_row[None, :] >= 0)
            & (position_row[None, :] < INTERVAL)
            & (position_row[None, :] < reach_row[:, None])
        )
        cache_mask = allowed[:, None, None, :]
        row_peak = jnp.max(jnp.where(cache_mask, scores, masked_score), axis=-1)
        weights = jnp.where(cache_mask, jnp.exp(scores - row_peak[..., None]), 0.0)
        weight_sum = jnp.sum(weights, axis=-1)
        weighted = jnp.einsum(
            "jkgi,ikd->jkgd",
            weights.astype(jnp.bfloat16),
            value_block,
            preferred_element_type=jnp.float32,
        )
        return (row_peak, weight_sum, weighted)

    return lax.map(per_request, (queries, key_rows, value_rows, positions, present, reaches))


def body(
    raw_keys,
    raw_values,
    phase,
    ratio,
    resident_len,
    beacon_queries,
    beacon_wk,
    beacon_wv,
    resident_keys,
    resident_values,
    decode_queries,
    out_weight,
):
    requests = raw_keys.shape[0]
    kv_local = raw_keys.shape[2]
    head_dim = raw_keys.shape[3]
    shard_index = lax.axis_index("seq")
    shard_count = lax.axis_size("seq")
    is_first = shard_index == 0
    is_last = shard_index == shard_count - 1
    own_ratio = lax.dynamic_index_in_dim(ratio, shard_index, 1, keepdims=False)
    slot_ids = jnp.arange(NB, dtype=jnp.int32)
    lead_in = jnp.where(is_first, phase, 0)
    reaches = (slot_ids[None, :] + 1) * own_ratio[:, None] + lead_in[:, None]
    tail_keys = raw_keys[:, INTERVAL - OFF :]
    tail_values = raw_values[:, INTERVAL - OFF :]
    own_positions = jnp.arange(INTERVAL, dtype=jnp.int32)[None, :] + phase[:, None]
    rim_ids = jnp.arange(OFF, dtype=jnp.int32)
    rim_positions = rim_ids[None, :] - OFF + phase[:, None]
    near_keys, near_values = shifted((tail_keys, tail_values), "seq", 1)
    key_rows = jnp.concatenate([near_keys, raw_keys], axis=1)
    value_rows = jnp.concatenate([near_values, raw_values], axis=1)
    positions = jnp.concatenate([rim_positions, own_positions], axis=1)
    present = jnp.logical_not(is_first) | (positions >= phase[:, None])
    pooled_parts = pool_part(beacon_queries, key_rows, value_rows, positions, present, reaches)
    pooled = (pooled_parts[2] / pooled_parts[1][..., None]).astype(jnp.bfloat16)
    pooled_flat = pooled.reshape(requests * NB, kv_local * G * head_dim)
    pooled_whole = lax.all_gather(pooled_flat, "head", axis=1, tiled=True)
    key_sum = jnp.dot(
        pooled_whole,
        lax.all_gather(beacon_wk, "seq", axis=0, tiled=True),
        preferred_element_type=jnp.float32,
    )
    value_sum = jnp.dot(
        pooled_whole,
        lax.all_gather(beacon_wv, "seq", axis=0, tiled=True),
        preferred_element_type=jnp.float32,
    )
    made_keys = key_sum
    made_values = value_sum
    made_keys = made_keys.reshape(requests, NB, kv_local, head_dim)
    made_values = made_values.reshape(requests, NB, kv_local, head_dim)
    slot_live = slot_ids[None, :] < (INTERVAL // own_ratio)[:, None]
    beacon_keys = jnp.where(slot_live[:, :, None, None], made_keys, 0.0).astype(jnp.bfloat16)
    beacon_values = jnp.where(slot_live[:, :, None, None], made_values, 0.0).astype(jnp.bfloat16)
    cache_keys = jnp.concatenate([resident_keys, beacon_keys, tail_keys], axis=1)
    cache_values = jnp.concatenate([resident_values, beacon_values, tail_values], axis=1)
    own_len = lax.dynamic_index_in_dim(resident_len, shard_index, 1, keepdims=False)
    resident_ok = jnp.arange(resident_keys.shape[1], dtype=jnp.int32)[None, :] < own_len[:, None]
    leftover_ok = (rim_ids[None, :] >= OFF - phase[:, None]) & is_last
    usable = jnp.concatenate([resident_ok, slot_live, leftover_ok], axis=1)
    inv_root = 1.0 / math.sqrt(head_dim)
    scores = (
        jnp.einsum(
            "srkgd,rikd->rksgi", decode_queries, cache_keys, preferred_element_type=jnp.float32
        )
        * inv_root
    )
    cache_mask = usable[:, None, None, None, :]
    row_peak = jnp.max(jnp.where(cache_mask, scores, masked_score), axis=-1)
    weights = jnp.where(cache_mask, jnp.exp(scores - row_peak[..., None]), 0.0)
    weight_sum = jnp.sum(weights, axis=-1)
    weighted = jnp.einsum(
        "rksgi,rikd->rksgd",
        weights.astype(jnp.bfloat16),
        cache_values,
        preferred_element_type=jnp.float32,
    )
    merged = joined((row_peak, weight_sum, weighted), "seq", blend)
    total_sum = merged[1]
    total_weighted = merged[2]
    attended = (total_weighted / total_sum[..., None]).astype(jnp.bfloat16)
    attended = jnp.transpose(attended, (2, 0, 1, 3, 4)).reshape(
        STEPS * requests, kv_local * G * head_dim
    )
    partial_value = jnp.dot(attended, out_weight, preferred_element_type=jnp.float32)
    summed = lax.psum(partial_value, "head")
    projected = summed.astype(jnp.bfloat16).reshape(STEPS, requests, out_weight.shape[1])
    return (beacon_keys, beacon_values, projected)


B = 4
CH = 4


def fused_kernel(
    shard_count,
    phase_ref,
    ratio_ref,
    rlen_ref,
    k_hbm,
    v_hbm,
    q_hbm,
    wk_hbm,
    wv_hbm,
    rk_ref,
    rv_ref,
    dq_ref,
    ow_hbm,
    bk_ref,
    bv_ref,
    proj_ref,
    kbuf,
    vbuf,
    qbuf,
    wbuf,
    act,
    stage,
    psend,
    precv,
    own,
    bias,
    owbuf,
    snd,
    snd_stats,
    rcv,
    rcv_stats,
    att,
    part,
    load_sem,
    rim_send,
    rim_recv,
    w_send,
    w_recv,
    a_send,
    a_recv,
    a_loc,
    p_send,
    p_recv,
    s_send,
    s_recv,
    d_send,
    d_recv,
    e_send,
    e_recv,
    t_send,
    t_recv,
    h_send,
    h_recv,
):
    n = shard_count
    depth = n // B
    s = lax.axis_index("seq")
    h = lax.axis_index("head")
    z = s // B
    me = lax.rem(s, B)
    heads, rows, hd = kbuf.shape[1], kbuf.shape[2], kbuf.shape[3]
    requests = kbuf.shape[0]
    interval = rows - OFF
    nb = bias.shape[1]
    width = wbuf.shape[3]
    inv_root = 1.0 / math.sqrt(hd)
    f32 = jnp.float32

    def remote(src, dst, send, recv, seq=None):
        target = {"head": 1 - h} if seq is None else {"seq": seq}
        return pltpu.make_async_remote_copy(
            src_ref=src,
            dst_ref=dst,
            send_sem=send,
            recv_sem=recv,
            device_id=target,
            device_id_type=pl.DeviceIdType.MESH,
        )

    loads = []
    half = wk_hbm.shape[1] // (CH // 2)
    for c in range(CH):
        source = (wk_hbm, wv_hbm)[c // (CH // 2)]
        first = (c % (CH // 2)) * half
        loads.append(
            pltpu.make_async_copy(
                source.at[:, first : first + half], wbuf.at[z, c], load_sem.at[c]
            )
        )
    loads.append(pltpu.make_async_copy(k_hbm, kbuf.at[:, :, OFF:], load_sem.at[CH]))
    loads.append(pltpu.make_async_copy(v_hbm, vbuf.at[:, :, OFF:], load_sem.at[CH + 1]))
    loads.append(pltpu.make_async_copy(q_hbm, qbuf, load_sem.at[CH + 2]))
    loads.append(pltpu.make_async_copy(ow_hbm, owbuf, load_sem.at[CH + 3]))
    for copy in loads:
        copy.start()

    barrier = pltpu.get_barrier_semaphore()
    for o in range(1, n):
        pl.semaphore_signal(
            barrier, inc=1, device_id={"seq": lax.rem(s + o, n)}, device_id_type=pl.DeviceIdType.MESH
        )
    pl.semaphore_signal(
        barrier, inc=1, device_id={"head": 1 - h}, device_id_type=pl.DeviceIdType.MESH
    )
    pl.semaphore_wait(barrier, n)

    def rim(which, k):
        source, target = ((k_hbm, kbuf), (v_hbm, vbuf))[which]
        return remote(
            source.at[:, k, interval - OFF :],
            target.at[:, k, :OFF],
            rim_send.at[which, k],
            rim_recv.at[which, k],
            lax.rem(s + 1, n),
        )

    @pl.when(s < n - 1)
    def _():
        for k in range(heads):
            rim(0, k).start()
            rim(1, k).start()

    @pl.when(s == 0)
    def _():
        kbuf[:, :, :OFF] = jnp.zeros((requests, heads, OFF, hd), kbuf.dtype)
        vbuf[:, :, :OFF] = jnp.zeros((requests, heads, OFF, hd), vbuf.dtype)

    def w_copy(way, d, c, shard, target):
        return remote(
            wbuf.at[shard, c],
            wbuf.at[shard, c],
            w_send.at[way, d, c],
            w_recv.at[way, d, c],
            target * B + me,
        )

    def w_out(way, d):
        if way == 0:
            return z - d, z + 1, (z - d >= 0) & (z + 1 < depth)
        return z + d, z - 1, (z + d < depth) & (z - 1 >= 0)

    def w_in(way, d):
        if way == 0:
            return z - 1 - d, z - 1 - d >= 0
        return z + 1 + d, z + 1 + d < depth

    def w_start(d, c):
        for way in range(2):
            shard, target, there = w_out(way, d)

            @pl.when(there)
            def _(way=way, shard=shard, target=target):
                w_copy(way, d, c, shard, target).start()

    def w_wait(d, c):
        for way in range(2):
            shard, there = w_in(way, d)

            @pl.when(there)
            def _(way=way, shard=shard):
                w_copy(way, d, c, shard, z).wait_recv()

    def w_relay(d, c):
        for way in range(2):
            shard, there = w_in(way, d - 1)
            out, target, onward = w_out(way, d)

            @pl.when(there)
            def _(way=way, shard=shard):
                w_copy(way, d - 1, c, shard, z).wait_recv()

            @pl.when(onward)
            def _(way=way, out=out, target=target):
                w_copy(way, d, c, out, target).start()

    def w_own(c):
        loads[c].wait()
        w_start(0, c)

    for c in range(CH):
        w_own(c)

    for r in range(requests):
        slot = lax.broadcasted_iota(jnp.int32, (nb, rows), 0)
        position = lax.broadcasted_iota(jnp.int32, (nb, rows), 1) - OFF + phase_ref[r]
        lead = jnp.where(s == 0, phase_ref[r], 0)
        reach = (slot + 1) * ratio_ref[r, s] + lead
        allowed = (position >= lead) & (position < interval) & (position < reach)
        bias[r] = jnp.where(allowed, 0.0, masked_score).astype(f32)

    loads[CH].wait()
    loads[CH + 1].wait()
    loads[CH + 2].wait()

    def a_remote(u, x):
        kk, r, y = u // 4, lax.rem(u, 2), lax.rem(u // 2, 2)
        return remote(
            stage.at[u, x],
            act.at[h * 2 + kk, me, r],
            a_send.at[u, x],
            a_recv.at[kk, r, me],
            z * B + y * 2 + x,
        )

    def a_local(kk, r, u):
        return pltpu.make_async_copy(
            stage.at[u, lax.rem(me, 2)], act.at[h * 2 + kk, me, r], a_loc.at[kk, r]
        )

    def a_relay(kk):
        return remote(
            act.at[h * 2 + kk], act.at[h * 2 + kk], p_send.at[kk], p_recv.at[kk]
        )

    def a_gather(kk):
        for r in range(requests):
            a_local(kk, r, kk * 4 + (me // 2) * 2 + r).wait()
            for o in range(1, B):
                source = lax.rem(me + o, B)
                remote(
                    stage.at[0, 0],
                    act.at[h * 2 + kk, source, r],
                    a_send.at[0, 0],
                    a_recv.at[kk, r, source],
                    s,
                ).wait_recv()
        a_relay(kk).start()

    def unit(u, carry):
        k, r = u // 2, lax.rem(u, 2)

        @pl.when((r == 0) & (s > 0))
        def _():
            rim(0, k).wait_recv()
            rim(1, k).wait_recv()

        for g in range(G):
            scores = (
                lax.dot_general(
                    qbuf[r, k, g],
                    kbuf[r, k],
                    (((1,), (1,)), ((), ())),
                    preferred_element_type=f32,
                )
                * inv_root
                + bias[r]
            )
            weights = jnp.exp(scores - jnp.max(scores, axis=-1, keepdims=True))
            total = jnp.sum(weights, axis=-1, keepdims=True)
            out = jnp.dot(weights.astype(jnp.bfloat16), vbuf[r, k], preferred_element_type=f32)
            at = (g % 4) * hd
            stage[u, g // 4, :, at : at + hd] = (out / total).astype(jnp.bfloat16)
        for x in range(2):
            member = lax.rem(k, 2) * 2 + x

            @pl.when(member == me)
            def _():
                a_local(u // 4, r, u).start()

            @pl.when(member != me)
            def _(x=x):
                a_remote(u, x).start()

        @pl.when(u == 3)
        def _():
            w_relay(1, 0)

        @pl.when(u == 6)
        def _():
            a_gather(0)

        return carry

    lax.fori_loop(0, 2 * heads, unit, 0)
    w_relay(2, 0)
    w_relay(1, 1)
    a_gather(1)
    w_relay(2, 1)
    w_relay(1, 2)
    a_relay(0).wait_recv()
    a_relay(1).wait_recv()

    def p_copy(c, to, frm):
        return remote(
            psend.at[to, c], precv.at[frm, c], s_send.at[to, c], s_recv.at[frm, c], z * B + to
        )

    slot_row = lax.broadcasted_iota(jnp.int32, (nb, width), 0)

    def finish(c):
        for o in range(1, B):
            source = lax.rem(me + o, B)
            p_copy(c, source, source).wait_recv()
        total = own[c]
        for o in range(1, B):
            total += precv[lax.rem(me + o, B), c].astype(f32)
        out_ref = (bk_ref, bv_ref)[c // (CH // 2)]
        at = (c % (CH // 2)) * width
        for r in range(requests):
            live = (slot_row + 1) * ratio_ref[r, s] <= interval
            out_ref[r * nb : (r + 1) * nb, at : at + width] = jnp.where(
                live, total[r * nb : (r + 1) * nb], 0.0
            ).astype(jnp.bfloat16)

    for c in range(CH):
        if c == 1:
            w_relay(2, 2)
            w_relay(1, 3)
        if c == 2:
            w_relay(2, 3)
        w_wait(depth - 2, c)

        def product(o, carry, c=c):
            to = lax.rem(me + 1 + o, B)
            total = jnp.zeros((requests * nb, width), f32)
            for zi in range(depth):
                total += jnp.dot(
                    act[zi, to].reshape(requests * nb, act.shape[4]),
                    wbuf[zi, c],
                    preferred_element_type=f32,
                )

            @pl.when(o < B - 1)
            def _():
                psend[to, c] = total.astype(jnp.bfloat16)
                p_copy(c, to, me).start()

            @pl.when(o == B - 1)
            def _():
                own[c] = total

            return carry

        lax.fori_loop(0, B, product, 0)
        if c > 0:
            finish(c - 1)
    finish(CH - 1)

    res = rk_ref.shape[2]
    qrows = dq_ref.shape[1]
    pair = qrows // G
    cells = res + nb + OFF
    row_request = lax.rem(lax.broadcasted_iota(jnp.int32, (qrows, cells), 0), pair) // (
        pair // requests
    )
    cell = lax.broadcasted_iota(jnp.int32, (qrows, cells), 1)
    last = jnp.where(s == n - 1, 1, 0)
    masks = []
    for r in range(requests):
        usable = (
            (cell < rlen_ref[r, s])
            | ((cell >= res) & (cell < res + nb) & ((cell - res + 1) * ratio_ref[r, s] <= interval))
            | ((cell >= res + nb + OFF - phase_ref[r] * last) & (cell >= res + nb))
        )
        masks.append(usable & (row_request == r))
    share = G * heads // n
    for k in range(heads):
        lanes = slice(k * hd, (k + 1) * hd)
        pieces = []
        for r in range(requests):
            keys = (rk_ref[r, k], bk_ref[r * nb : (r + 1) * nb, lanes], kbuf[r, k, rows - OFF :])
            scores = jnp.concatenate(
                [
                    lax.dot_general(
                        dq_ref[k], key, (((1,), (1,)), ((), ())), preferred_element_type=f32
                    )
                    for key in keys
                ],
                axis=1,
            )
            pieces.append(jnp.where(masks[r], scores * inv_root, masked_score))
        peak = jnp.maximum(
            jnp.max(pieces[0], axis=-1, keepdims=True), jnp.max(pieces[1], axis=-1, keepdims=True)
        )
        total = jnp.zeros((qrows, 1), f32)
        out = jnp.zeros((qrows, hd), f32)
        for r in range(requests):
            weights = jnp.exp(pieces[r] - peak)
            total += jnp.sum(weights, axis=-1, keepdims=True)
            low = weights.astype(jnp.bfloat16)
            out += jnp.dot(low[:, :res], rv_ref[r, k], preferred_element_type=f32)
            out += jnp.dot(
                low[:, res : res + nb],
                bv_ref[r * nb : (r + 1) * nb, lanes],
                preferred_element_type=f32,
            )
            out += jnp.dot(
                low[:, res + nb :], vbuf[r, k, rows - OFF :], preferred_element_type=f32
            )
        lane = lax.broadcasted_iota(jnp.int32, (qrows, hd), 1)
        slots = hd // (2 * share)
        stats = jnp.where(lax.rem(lane // slots, 2) == 0, peak, total)
        stats = stats.reshape(G // share, share, pair, hd)
        lane = lax.broadcasted_iota(jnp.int32, (G // share, pair, hd), 2)
        packed = stats[:, 0]
        for j in range(1, share):
            packed = jnp.where(lane >= 2 * slots * j, stats[:, j], packed)
        dests = slice(k * G // share, (k + 1) * G // share)
        snd[dests] = out.reshape(G // share, share * pair, hd).astype(jnp.bfloat16)
        snd_stats[dests] = packed

    def d_copy(to, frm):
        return remote(snd.at[to], rcv.at[frm], d_send.at[to], d_recv.at[frm], to)

    def e_copy(to, frm):
        return remote(snd_stats.at[to], rcv_stats.at[frm], e_send.at[to], e_recv.at[frm], to)

    def t_copy(to, frm):
        return remote(att.at[frm], att.at[frm], t_send.at[to], t_recv.at[frm], to)

    for o in range(1, n):
        e_copy(lax.rem(s + o, n), s).start()
        d_copy(lax.rem(s + o, n), s).start()
    rcv[s] = snd[s]
    rcv_stats[s] = snd_stats[s]
    for o in range(1, n):
        source = lax.rem(s + o, n)
        e_copy(source, source).wait_recv()
        d_copy(source, source).wait_recv()
    landed = rcv[...].astype(f32)
    attended = []
    for j in range(share):
        at = 2 * slots * j
        peaks = rcv_stats[:, :, at : at + 1]
        sums = rcv_stats[:, :, at + slots : at + slots + 1]
        scale = jnp.exp(peaks - jnp.max(peaks, axis=0, keepdims=True))
        mixed = jnp.sum(scale * landed[:, j * pair : (j + 1) * pair], axis=0)
        attended.append(mixed / jnp.sum(scale * sums, axis=0))
    att[s] = jnp.concatenate(attended, axis=0).astype(jnp.bfloat16)
    for o in range(1, n):
        t_copy(lax.rem(s + o, n), s).start()
    for o in range(1, n):
        source = lax.rem(s + o, n)
        t_copy(source, source).wait_recv()
    loads[CH + 3].wait()
    wide = [att[i].astype(f32) for i in range(n)]
    vectors = jnp.concatenate(
        [wide[i][j * pair : (j + 1) * pair] for i in range(n) for j in range(share)], axis=1
    ).astype(jnp.bfloat16)
    partial_value = jnp.dot(vectors, owbuf[...], preferred_element_type=f32)
    part[0] = partial_value
    swap = remote(part.at[0], part.at[1], h_send, h_recv)
    swap.start()
    swap.wait_recv()
    first = jnp.where(h == 0, part[0], part[1])
    second = jnp.where(h == 0, part[1], part[0])
    proj_ref[...] = (first + second).astype(jnp.bfloat16)

    swap.wait_send()
    for o in range(1, n):
        d_copy(lax.rem(s + o, n), s).wait_send()
        e_copy(lax.rem(s + o, n), s).wait_send()
        t_copy(lax.rem(s + o, n), s).wait_send()
    for c in range(CH):
        for o in range(1, B):
            p_copy(c, lax.rem(me + o, B), me).wait_send()
    a_relay(0).wait_send()
    a_relay(1).wait_send()
    for u in range(2 * heads):
        for x in range(2):

            @pl.when((u // 2 % 2) * 2 + x != me)
            def _(u=u, x=x):
                a_remote(jnp.int32(u), x).wait_send()

    for way in range(2):
        for d in range(depth - 1):
            shard, target, there = w_out(way, d)
            for c in range(CH):

                @pl.when(there)
                def _(way=way, d=d, c=c, shard=shard, target=target):
                    w_copy(way, d, c, shard, target).wait_send()

    @pl.when(s < n - 1)
    def _():
        for k in range(heads):
            rim(0, k).wait_send()
            rim(1, k).wait_send()


def fused_body(
    shard_count,
    raw_keys,
    raw_values,
    phase,
    ratio,
    resident_len,
    beacon_queries,
    beacon_wk,
    beacon_wv,
    resident_keys,
    resident_values,
    decode_queries,
    out_weight,
):
    n = shard_count
    depth = n // B
    requests, interval, heads, hd = raw_keys.shape
    steps = decode_queries.shape[0]
    nb = beacon_queries.shape[1]
    rows = interval + OFF
    by_head = (0, 2, 1, 3)
    feature, columns = beacon_wk.shape
    width = 2 * columns // CH
    pair = requests * steps
    share = G * heads // n
    bf16, f32 = jnp.bfloat16, jnp.float32
    dma = pltpu.SemaphoreType.DMA
    smem = pl.BlockSpec(memory_space=pltpu.SMEM)
    anywhere = pl.BlockSpec(memory_space=pl.ANY)
    vmem = pl.BlockSpec(memory_space=pltpu.VMEM)
    keys, values, projected = pl.pallas_call(
        functools.partial(fused_kernel, n),
        out_shape=(
            jax.ShapeDtypeStruct((requests * nb, columns), bf16),
            jax.ShapeDtypeStruct((requests * nb, columns), bf16),
            jax.ShapeDtypeStruct((pair, out_weight.shape[1]), bf16),
        ),
        in_specs=[smem] * 3 + [anywhere] * 5 + [vmem] * 3 + [anywhere],
        out_specs=(vmem, vmem, vmem),
        scratch_shapes=[
            pltpu.VMEM((requests, heads, rows, hd), bf16),
            pltpu.VMEM((requests, heads, rows, hd), bf16),
            pltpu.VMEM((requests, heads, G, nb, hd), bf16),
            pltpu.VMEM((depth, CH, feature, width), bf16),
            pltpu.VMEM((depth, B, requests, nb, feature), bf16),
            pltpu.VMEM((requests * heads, 2, nb, feature), bf16),
            pltpu.VMEM((B, CH, requests * nb, width), bf16),
            pltpu.VMEM((B, CH, requests * nb, width), bf16),
            pltpu.VMEM((CH, requests * nb, width), f32),
            pltpu.VMEM((requests, nb, rows), f32),
            pltpu.VMEM(out_weight.shape, bf16),
            pltpu.VMEM((n, share * pair, hd), bf16),
            pltpu.VMEM((n, pair, hd), f32),
            pltpu.VMEM((n, share * pair, hd), bf16),
            pltpu.VMEM((n, pair, hd), f32),
            pltpu.VMEM((n, share * pair, hd), bf16),
            pltpu.VMEM((2, pair, out_weight.shape[1]), f32),
            dma((CH + 4,)),
            dma((2, heads)),
            dma((2, heads)),
            dma((2, depth - 1, CH)),
            dma((2, depth - 1, CH)),
            dma((requests * heads, 2)),
            dma((2, requests, B)),
            dma((2, requests)),
            dma((2,)),
            dma((2,)),
            dma((B, CH)),
            dma((B, CH)),
            dma((n,)),
            dma((n,)),
            dma((n,)),
            dma((n,)),
            dma((n,)),
            dma((n,)),
            dma,
            dma,
        ],
        compiler_params=pltpu.CompilerParams(
            collective_id=0, has_side_effects=True, vmem_limit_bytes=60 * 1024 * 1024
        ),
    )(
        phase,
        ratio,
        resident_len,
        jnp.transpose(raw_keys, by_head),
        jnp.transpose(raw_values, by_head),
        jnp.transpose(beacon_queries, (0, 2, 3, 1, 4)),
        beacon_wk,
        beacon_wv,
        jnp.transpose(resident_keys, by_head),
        jnp.transpose(resident_values, by_head),
        jnp.transpose(decode_queries, (2, 3, 1, 0, 4)).reshape(heads, G * pair, hd),
        out_weight,
    )
    return (
        keys.reshape(requests, nb, heads, hd),
        values.reshape(requests, nb, heads, hd),
        jnp.transpose(projected.reshape(requests, steps, -1), (1, 0, 2)),
    )


def chosen_body(shard_count, head_count):
    def run(*arrays):
        requests, _, heads, hd = arrays[0].shape
        feature = arrays[6].shape[0]
        fits = (
            head_count == 2
            and shard_count == B * B
            and requests == 2
            and heads == B
            and 2 * feature == G * hd
        )
        return fused_body(shard_count, *arrays) if fits else body(*arrays)

    return run


def solution(mesh):
    return jax.shard_map(
        chosen_body(mesh.shape["seq"], mesh.shape["head"]),
        mesh=mesh,
        in_specs=(
            P(None, "seq", "head", None),
            P(None, "seq", "head", None),
            P(),
            P(),
            P(),
            P(None, "seq", "head", None, None),
            P("seq", "head"),
            P("seq", "head"),
            P(None, "seq", "head", None),
            P(None, "seq", "head", None),
            P(None, None, "head", None, None),
            P("head", "seq"),
        ),
        out_specs=(
            P(None, "seq", "head", None),
            P(None, "seq", "head", None),
            P(None, None, "seq"),
        ),
        check_vma=False,
    )
```

```python
import functools
import math

import jax
import jax.numpy as jnp
from jax import lax
from jax.experimental import pallas as pl
from jax.experimental.pallas import tpu as pltpu
from jax.sharding import PartitionSpec as P

G = 8
INTERVAL = 1024
NB = 128
OFF = 256
STEPS = 4


masked_score = -1e30


def shifted(value, axis, steps):
    count = lax.axis_size(axis)
    first, last = (max(0, -steps), min(count, count - steps))
    return lax.ppermute(value, axis, [(source, source + steps) for source in range(first, last)])


def joined(shard, axis, combine):
    everything = jax.tree.map(lambda part: lax.all_gather(part, axis), shard)
    first = jax.tree.map(lambda part: part[0], everything)

    def hop(k, so_far):
        return combine(so_far, jax.tree.map(lambda part: part[k], everything))

    return lax.fori_loop(1, lax.axis_size(axis), hop, first)


def blend(former, latter):
    row_peak = jnp.maximum(former[0], latter[0])
    former_scale = jnp.exp(former[0] - row_peak)
    latter_scale = jnp.exp(latter[0] - row_peak)
    weight_sum = former[1] * former_scale + latter[1] * latter_scale
    weighted = former[2] * former_scale[..., None] + latter[2] * latter_scale[..., None]
    return (row_peak, weight_sum, weighted)


def pool_part(queries, key_rows, value_rows, positions, present, reaches):
    inv_root = 1.0 / math.sqrt(queries.shape[-1])

    def per_request(members):
        query_block, key_block, value_block, position_row, present_row, reach_row = members
        scores = (
            jnp.einsum("jkgd,ikd->jkgi", query_block, key_block, preferred_element_type=jnp.float32)
            * inv_root
        )
        allowed = (
            present_row[None, :]
            & (position_row[None, :] >= 0)
            & (position_row[None, :] < INTERVAL)
            & (position_row[None, :] < reach_row[:, None])
        )
        cache_mask = allowed[:, None, None, :]
        row_peak = jnp.max(jnp.where(cache_mask, scores, masked_score), axis=-1)
        weights = jnp.where(cache_mask, jnp.exp(scores - row_peak[..., None]), 0.0)
        weight_sum = jnp.sum(weights, axis=-1)
        weighted = jnp.einsum(
            "jkgi,ikd->jkgd",
            weights.astype(jnp.bfloat16),
            value_block,
            preferred_element_type=jnp.float32,
        )
        return (row_peak, weight_sum, weighted)

    return lax.map(per_request, (queries, key_rows, value_rows, positions, present, reaches))


def body(
    raw_keys,
    raw_values,
    phase,
    ratio,
    resident_len,
    beacon_queries,
    beacon_wk,
    beacon_wv,
    resident_keys,
    resident_values,
    decode_queries,
    out_weight,
):
    requests = raw_keys.shape[0]
    kv_local = raw_keys.shape[2]
    head_dim = raw_keys.shape[3]
    shard_index = lax.axis_index("seq")
    shard_count = lax.axis_size("seq")
    is_first = shard_index == 0
    is_last = shard_index == shard_count - 1
    own_ratio = lax.dynamic_index_in_dim(ratio, shard_index, 1, keepdims=False)
    slot_ids = jnp.arange(NB, dtype=jnp.int32)
    lead_in = jnp.where(is_first, phase, 0)
    reaches = (slot_ids[None, :] + 1) * own_ratio[:, None] + lead_in[:, None]
    tail_keys = raw_keys[:, INTERVAL - OFF :]
    tail_values = raw_values[:, INTERVAL - OFF :]
    own_positions = jnp.arange(INTERVAL, dtype=jnp.int32)[None, :] + phase[:, None]
    rim_ids = jnp.arange(OFF, dtype=jnp.int32)
    rim_positions = rim_ids[None, :] - OFF + phase[:, None]
    near_keys, near_values = shifted((tail_keys, tail_values), "seq", 1)
    key_rows = jnp.concatenate([near_keys, raw_keys], axis=1)
    value_rows = jnp.concatenate([near_values, raw_values], axis=1)
    positions = jnp.concatenate([rim_positions, own_positions], axis=1)
    present = jnp.logical_not(is_first) | (positions >= phase[:, None])
    pooled_parts = pool_part(beacon_queries, key_rows, value_rows, positions, present, reaches)
    pooled = (pooled_parts[2] / pooled_parts[1][..., None]).astype(jnp.bfloat16)
    pooled_flat = pooled.reshape(requests * NB, kv_local * G * head_dim)
    pooled_whole = lax.all_gather(pooled_flat, "head", axis=1, tiled=True)
    key_sum = jnp.dot(
        pooled_whole,
        lax.all_gather(beacon_wk, "seq", axis=0, tiled=True),
        preferred_element_type=jnp.float32,
    )
    value_sum = jnp.dot(
        pooled_whole,
        lax.all_gather(beacon_wv, "seq", axis=0, tiled=True),
        preferred_element_type=jnp.float32,
    )
    made_keys = key_sum
    made_values = value_sum
    made_keys = made_keys.reshape(requests, NB, kv_local, head_dim)
    made_values = made_values.reshape(requests, NB, kv_local, head_dim)
    slot_live = slot_ids[None, :] < (INTERVAL // own_ratio)[:, None]
    beacon_keys = jnp.where(slot_live[:, :, None, None], made_keys, 0.0).astype(jnp.bfloat16)
    beacon_values = jnp.where(slot_live[:, :, None, None], made_values, 0.0).astype(jnp.bfloat16)
    cache_keys = jnp.concatenate([resident_keys, beacon_keys, tail_keys], axis=1)
    cache_values = jnp.concatenate([resident_values, beacon_values, tail_values], axis=1)
    own_len = lax.dynamic_index_in_dim(resident_len, shard_index, 1, keepdims=False)
    resident_ok = jnp.arange(resident_keys.shape[1], dtype=jnp.int32)[None, :] < own_len[:, None]
    leftover_ok = (rim_ids[None, :] >= OFF - phase[:, None]) & is_last
    usable = jnp.concatenate([resident_ok, slot_live, leftover_ok], axis=1)
    inv_root = 1.0 / math.sqrt(head_dim)
    scores = (
        jnp.einsum(
            "srkgd,rikd->rksgi", decode_queries, cache_keys, preferred_element_type=jnp.float32
        )
        * inv_root
    )
    cache_mask = usable[:, None, None, None, :]
    row_peak = jnp.max(jnp.where(cache_mask, scores, masked_score), axis=-1)
    weights = jnp.where(cache_mask, jnp.exp(scores - row_peak[..., None]), 0.0)
    weight_sum = jnp.sum(weights, axis=-1)
    weighted = jnp.einsum(
        "rksgi,rikd->rksgd",
        weights.astype(jnp.bfloat16),
        cache_values,
        preferred_element_type=jnp.float32,
    )
    merged = joined((row_peak, weight_sum, weighted), "seq", blend)
    total_sum = merged[1]
    total_weighted = merged[2]
    attended = (total_weighted / total_sum[..., None]).astype(jnp.bfloat16)
    attended = jnp.transpose(attended, (2, 0, 1, 3, 4)).reshape(
        STEPS * requests, kv_local * G * head_dim
    )
    partial_value = jnp.dot(attended, out_weight, preferred_element_type=jnp.float32)
    summed = lax.psum(partial_value, "head")
    projected = summed.astype(jnp.bfloat16).reshape(STEPS, requests, out_weight.shape[1])
    return (beacon_keys, beacon_values, projected)


B = 4
CH = 4


def fused_kernel(
    shard_count,
    phase_ref,
    ratio_ref,
    rlen_ref,
    k_hbm,
    v_hbm,
    q_hbm,
    wk_hbm,
    wv_hbm,
    rk_raw,
    rv_raw,
    dq_ref,
    ow_hbm,
    bk_ref,
    bv_ref,
    proj_ref,
    kbuf,
    vbuf,
    qbuf,
    wbuf,
    act,
    stage,
    psend,
    precv,
    own,
    bias,
    owbuf,
    rk_ref,
    rv_ref,
    snd,
    snd_stats,
    rcv,
    rcv_stats,
    att,
    part,
    load_sem,
    rim_send,
    rim_recv,
    w_send,
    w_recv,
    a_send,
    a_recv,
    a_loc,
    p_send,
    p_recv,
    s_send,
    s_recv,
    d_send,
    d_recv,
    e_send,
    e_recv,
    t_send,
    t_recv,
    h_send,
    h_recv,
):
    n = shard_count
    depth = n // B
    s = lax.axis_index("seq")
    h = lax.axis_index("head")
    z = s // B
    me = lax.rem(s, B)
    heads, rows, hd = kbuf.shape[1], kbuf.shape[2], kbuf.shape[3]
    requests = kbuf.shape[0]
    interval = rows - OFF
    nb = bias.shape[1]
    width = wbuf.shape[3]
    inv_root = 1.0 / math.sqrt(hd)
    f32 = jnp.float32

    def remote(src, dst, send, recv, seq=None):
        target = {"head": 1 - h} if seq is None else {"seq": seq}
        return pltpu.make_async_remote_copy(
            src_ref=src,
            dst_ref=dst,
            send_sem=send,
            recv_sem=recv,
            device_id=target,
            device_id_type=pl.DeviceIdType.MESH,
        )

    loads = []
    half = wk_hbm.shape[1] // (CH // 2)
    for c in range(CH):
        source = (wk_hbm, wv_hbm)[c // (CH // 2)]
        first = (c % (CH // 2)) * half
        loads.append(
            pltpu.make_async_copy(
                source.at[:, first : first + half], wbuf.at[z, c], load_sem.at[c]
            )
        )
    loads.append(pltpu.make_async_copy(k_hbm, kbuf.at[:, :, OFF:], load_sem.at[CH]))
    loads.append(pltpu.make_async_copy(v_hbm, vbuf.at[:, :, OFF:], load_sem.at[CH + 1]))
    loads.append(pltpu.make_async_copy(q_hbm, qbuf, load_sem.at[CH + 2]))
    loads.append(pltpu.make_async_copy(ow_hbm, owbuf, load_sem.at[CH + 3]))
    for copy in loads:
        copy.start()

    barrier = pltpu.get_barrier_semaphore()
    for o in range(1, n):
        pl.semaphore_signal(
            barrier, inc=1, device_id={"seq": lax.rem(s + o, n)}, device_id_type=pl.DeviceIdType.MESH
        )
    pl.semaphore_signal(
        barrier, inc=1, device_id={"head": 1 - h}, device_id_type=pl.DeviceIdType.MESH
    )
    pl.semaphore_wait(barrier, n)

    def rim(which, k):
        source, target = ((k_hbm, kbuf), (v_hbm, vbuf))[which]
        return remote(
            source.at[:, k, interval - OFF :],
            target.at[:, k, :OFF],
            rim_send.at[which, k],
            rim_recv.at[which, k],
            lax.rem(s + 1, n),
        )

    @pl.when(s < n - 1)
    def _():
        for k in range(heads):
            rim(0, k).start()
            rim(1, k).start()

    @pl.when(s == 0)
    def _():
        kbuf[:, :, :OFF] = jnp.zeros((requests, heads, OFF, hd), kbuf.dtype)
        vbuf[:, :, :OFF] = jnp.zeros((requests, heads, OFF, hd), vbuf.dtype)

    def w_copy(way, d, c, shard, target):
        return remote(
            wbuf.at[shard, c],
            wbuf.at[shard, c],
            w_send.at[way, d, c],
            w_recv.at[way, d, c],
            target * B + me,
        )

    def w_out(way, d):
        if way == 0:
            return z - d, z + 1, (z - d >= 0) & (z + 1 < depth)
        return z + d, z - 1, (z + d < depth) & (z - 1 >= 0)

    def w_in(way, d):
        if way == 0:
            return z - 1 - d, z - 1 - d >= 0
        return z + 1 + d, z + 1 + d < depth

    def w_start(d, c):
        for way in range(2):
            shard, target, there = w_out(way, d)

            @pl.when(there)
            def _(way=way, shard=shard, target=target):
                w_copy(way, d, c, shard, target).start()

    def w_wait(d, c):
        for way in range(2):
            shard, there = w_in(way, d)

            @pl.when(there)
            def _(way=way, shard=shard):
                w_copy(way, d, c, shard, z).wait_recv()

    def w_relay(d, c):
        for way in range(2):
            shard, there = w_in(way, d - 1)
            out, target, onward = w_out(way, d)

            @pl.when(there)
            def _(way=way, shard=shard):
                w_copy(way, d - 1, c, shard, z).wait_recv()

            @pl.when(onward)
            def _(way=way, out=out, target=target):
                w_copy(way, d, c, out, target).start()

    def w_own(c):
        loads[c].wait()
        w_start(0, c)

    for c in range(CH):
        w_own(c)

    for r in range(requests):
        slot = lax.broadcasted_iota(jnp.int32, (nb, rows), 0)
        position = lax.broadcasted_iota(jnp.int32, (nb, rows), 1) - OFF + phase_ref[r]
        lead = jnp.where(s == 0, phase_ref[r], 0)
        reach = (slot + 1) * ratio_ref[r, s] + lead
        allowed = (position >= lead) & (position < interval) & (position < reach)
        bias[r] = jnp.where(allowed, 0.0, masked_score).astype(f32)

    loads[CH].wait()
    loads[CH + 1].wait()
    loads[CH + 2].wait()

    def a_remote(u, x):
        kk, r, y = u // 4, lax.rem(u, 2), lax.rem(u // 2, 2)
        return remote(
            stage.at[u, x],
            act.at[h * 2 + kk, me, r],
            a_send.at[u, x],
            a_recv.at[kk, r, me],
            z * B + y * 2 + x,
        )

    def a_local(kk, r, u):
        return pltpu.make_async_copy(
            stage.at[u, lax.rem(me, 2)], act.at[h * 2 + kk, me, r], a_loc.at[kk, r]
        )

    def a_relay(kk):
        return remote(
            act.at[h * 2 + kk], act.at[h * 2 + kk], p_send.at[kk], p_recv.at[kk]
        )

    def a_gather(kk):
        for r in range(requests):
            a_local(kk, r, kk * 4 + (me // 2) * 2 + r).wait()
            for o in range(1, B):
                source = lax.rem(me + o, B)
                remote(
                    stage.at[0, 0],
                    act.at[h * 2 + kk, source, r],
                    a_send.at[0, 0],
                    a_recv.at[kk, r, source],
                    s,
                ).wait_recv()
        a_relay(kk).start()

    def unit(u, carry):
        k, r = u // 2, lax.rem(u, 2)

        @pl.when((r == 0) & (s > 0))
        def _():
            rim(0, k).wait_recv()
            rim(1, k).wait_recv()

        for g in range(G):
            scores = (
                lax.dot_general(
                    qbuf[r, k, g],
                    kbuf[r, k],
                    (((1,), (1,)), ((), ())),
                    preferred_element_type=f32,
                )
                * inv_root
                + bias[r]
            )
            weights = jnp.exp(scores - jnp.max(scores, axis=-1, keepdims=True))
            total = jnp.sum(weights, axis=-1, keepdims=True)
            out = jnp.dot(weights.astype(jnp.bfloat16), vbuf[r, k], preferred_element_type=f32)
            at = (g % 4) * hd
            stage[u, g // 4, :, at : at + hd] = (out / total).astype(jnp.bfloat16)
        for x in range(2):
            member = lax.rem(k, 2) * 2 + x

            @pl.when(member == me)
            def _():
                a_local(u // 4, r, u).start()

            @pl.when(member != me)
            def _(x=x):
                a_remote(u, x).start()

        @pl.when(u == 3)
        def _():
            w_relay(1, 0)

        @pl.when(u == 6)
        def _():
            a_gather(0)

        return carry

    lax.fori_loop(0, 2 * heads, unit, 0)
    w_relay(2, 0)
    w_relay(1, 1)
    for r in range(requests):
        rk_ref[r] = jnp.swapaxes(rk_raw[r], 0, 1)
        rv_ref[r] = jnp.swapaxes(rv_raw[r], 0, 1)
    a_gather(1)
    w_relay(2, 1)
    w_relay(1, 2)
    a_relay(0).wait_recv()
    a_relay(1).wait_recv()

    def p_copy(c, to, frm):
        return remote(
            psend.at[to, c], precv.at[frm, c], s_send.at[to, c], s_recv.at[frm, c], z * B + to
        )

    slot_row = lax.broadcasted_iota(jnp.int32, (nb, width), 0)

    def finish(c):
        for o in range(1, B):
            source = lax.rem(me + o, B)
            p_copy(c, source, source).wait_recv()
        total = own[c]
        for o in range(1, B):
            total += precv[lax.rem(me + o, B), c].astype(f32)
        out_ref = (bk_ref, bv_ref)[c // (CH // 2)]
        at = (c % (CH // 2)) * width
        for r in range(requests):
            live = (slot_row + 1) * ratio_ref[r, s] <= interval
            out_ref[r * nb : (r + 1) * nb, at : at + width] = jnp.where(
                live, total[r * nb : (r + 1) * nb], 0.0
            ).astype(jnp.bfloat16)

    for c in range(CH):
        if c == 1:
            w_relay(2, 2)
            w_relay(1, 3)
        if c == 2:
            w_relay(2, 3)
        w_wait(depth - 2, c)

        def product(o, carry, c=c):
            to = lax.rem(me + 1 + o, B)
            total = jnp.zeros((requests * nb, width), f32)
            for zi in range(depth):
                total += jnp.dot(
                    act[zi, to].reshape(requests * nb, act.shape[4]),
                    wbuf[zi, c],
                    preferred_element_type=f32,
                )

            @pl.when(o < B - 1)
            def _():
                psend[to, c] = total.astype(jnp.bfloat16)
                p_copy(c, to, me).start()

            @pl.when(o == B - 1)
            def _():
                own[c] = total

            return carry

        lax.fori_loop(0, B, product, 0)
        if c > 0:
            finish(c - 1)
    finish(CH - 1)

    res = rk_ref.shape[2]
    qrows = dq_ref.shape[1]
    pair = qrows // G
    cells = res + nb + OFF
    row_request = lax.rem(lax.broadcasted_iota(jnp.int32, (qrows, cells), 0), pair) // (
        pair // requests
    )
    cell = lax.broadcasted_iota(jnp.int32, (qrows, cells), 1)
    last = jnp.where(s == n - 1, 1, 0)
    masks = []
    for r in range(requests):
        usable = (
            (cell < rlen_ref[r, s])
            | ((cell >= res) & (cell < res + nb) & ((cell - res + 1) * ratio_ref[r, s] <= interval))
            | ((cell >= res + nb + OFF - phase_ref[r] * last) & (cell >= res + nb))
        )
        masks.append(usable & (row_request == r))
    share = G * heads // n
    for k in range(heads):
        lanes = slice(k * hd, (k + 1) * hd)
        pieces = []
        for r in range(requests):
            keys = (rk_ref[r, k], bk_ref[r * nb : (r + 1) * nb, lanes], kbuf[r, k, rows - OFF :])
            scores = jnp.concatenate(
                [
                    lax.dot_general(
                        dq_ref[k], key, (((1,), (1,)), ((), ())), preferred_element_type=f32
                    )
                    for key in keys
                ],
                axis=1,
            )
            pieces.append(jnp.where(masks[r], scores * inv_root, masked_score))
        peak = jnp.maximum(
            jnp.max(pieces[0], axis=-1, keepdims=True), jnp.max(pieces[1], axis=-1, keepdims=True)
        )
        total = jnp.zeros((qrows, 1), f32)
        out = jnp.zeros((qrows, hd), f32)
        for r in range(requests):
            weights = jnp.exp(pieces[r] - peak)
            total += jnp.sum(weights, axis=-1, keepdims=True)
            low = weights.astype(jnp.bfloat16)
            out += jnp.dot(low[:, :res], rv_ref[r, k], preferred_element_type=f32)
            out += jnp.dot(
                low[:, res : res + nb],
                bv_ref[r * nb : (r + 1) * nb, lanes],
                preferred_element_type=f32,
            )
            out += jnp.dot(
                low[:, res + nb :], vbuf[r, k, rows - OFF :], preferred_element_type=f32
            )
        lane = lax.broadcasted_iota(jnp.int32, (qrows, hd), 1)
        slots = hd // (2 * share)
        stats = jnp.where(lax.rem(lane // slots, 2) == 0, peak, total)
        stats = stats.reshape(G // share, share, pair, hd)
        lane = lax.broadcasted_iota(jnp.int32, (G // share, pair, hd), 2)
        packed = stats[:, 0]
        for j in range(1, share):
            packed = jnp.where(lane >= 2 * slots * j, stats[:, j], packed)
        dests = slice(k * G // share, (k + 1) * G // share)
        snd[dests] = out.reshape(G // share, share * pair, hd).astype(jnp.bfloat16)
        snd_stats[dests] = packed

    def d_copy(to, frm):
        return remote(snd.at[to], rcv.at[frm], d_send.at[to], d_recv.at[frm], to)

    def e_copy(to, frm):
        return remote(snd_stats.at[to], rcv_stats.at[frm], e_send.at[to], e_recv.at[frm], to)

    def t_copy(to, frm):
        return remote(att.at[frm], att.at[frm], t_send.at[to], t_recv.at[frm], to)

    for o in range(1, n):
        e_copy(lax.rem(s + o, n), s).start()
        d_copy(lax.rem(s + o, n), s).start()
    rcv[s] = snd[s]
    rcv_stats[s] = snd_stats[s]
    for o in range(1, n):
        source = lax.rem(s + o, n)
        e_copy(source, source).wait_recv()
        d_copy(source, source).wait_recv()
    landed = rcv[...].astype(f32)
    attended = []
    for j in range(share):
        at = 2 * slots * j
        peaks = rcv_stats[:, :, at : at + 1]
        sums = rcv_stats[:, :, at + slots : at + slots + 1]
        scale = jnp.exp(peaks - jnp.max(peaks, axis=0, keepdims=True))
        mixed = jnp.sum(scale * landed[:, j * pair : (j + 1) * pair], axis=0)
        attended.append(mixed / jnp.sum(scale * sums, axis=0))
    att[s] = jnp.concatenate(attended, axis=0).astype(jnp.bfloat16)
    for o in range(1, n):
        t_copy(lax.rem(s + o, n), s).start()
    for o in range(1, n):
        source = lax.rem(s + o, n)
        t_copy(source, source).wait_recv()
    loads[CH + 3].wait()
    wide = [att[i].astype(f32) for i in range(n)]
    vectors = jnp.concatenate(
        [wide[i][j * pair : (j + 1) * pair] for i in range(n) for j in range(share)], axis=1
    ).astype(jnp.bfloat16)
    partial_value = jnp.dot(vectors, owbuf[...], preferred_element_type=f32)
    part[0] = partial_value
    swap = remote(part.at[0], part.at[1], h_send, h_recv)
    swap.start()
    swap.wait_recv()
    first = jnp.where(h == 0, part[0], part[1])
    second = jnp.where(h == 0, part[1], part[0])
    proj_ref[...] = (first + second).astype(jnp.bfloat16)

    swap.wait_send()
    for o in range(1, n):
        d_copy(lax.rem(s + o, n), s).wait_send()
        e_copy(lax.rem(s + o, n), s).wait_send()
        t_copy(lax.rem(s + o, n), s).wait_send()
    for c in range(CH):
        for o in range(1, B):
            p_copy(c, lax.rem(me + o, B), me).wait_send()
    a_relay(0).wait_send()
    a_relay(1).wait_send()
    for u in range(2 * heads):
        for x in range(2):

            @pl.when((u // 2 % 2) * 2 + x != me)
            def _(u=u, x=x):
                a_remote(jnp.int32(u), x).wait_send()

    for way in range(2):
        for d in range(depth - 1):
            shard, target, there = w_out(way, d)
            for c in range(CH):

                @pl.when(there)
                def _(way=way, d=d, c=c, shard=shard, target=target):
                    w_copy(way, d, c, shard, target).wait_send()

    @pl.when(s < n - 1)
    def _():
        for k in range(heads):
            rim(0, k).wait_send()
            rim(1, k).wait_send()


def fused_body(
    shard_count,
    raw_keys,
    raw_values,
    phase,
    ratio,
    resident_len,
    beacon_queries,
    beacon_wk,
    beacon_wv,
    resident_keys,
    resident_values,
    decode_queries,
    out_weight,
):
    n = shard_count
    depth = n // B
    requests, interval, heads, hd = raw_keys.shape
    steps = decode_queries.shape[0]
    nb = beacon_queries.shape[1]
    rows = interval + OFF
    by_head = (0, 2, 1, 3)
    feature, columns = beacon_wk.shape
    width = 2 * columns // CH
    pair = requests * steps
    share = G * heads // n
    bf16, f32 = jnp.bfloat16, jnp.float32
    dma = pltpu.SemaphoreType.DMA
    smem = pl.BlockSpec(memory_space=pltpu.SMEM)
    anywhere = pl.BlockSpec(memory_space=pl.ANY)
    vmem = pl.BlockSpec(memory_space=pltpu.VMEM)
    keys, values, projected = pl.pallas_call(
        functools.partial(fused_kernel, n),
        out_shape=(
            jax.ShapeDtypeStruct((requests * nb, columns), bf16),
            jax.ShapeDtypeStruct((requests * nb, columns), bf16),
            jax.ShapeDtypeStruct((pair, out_weight.shape[1]), bf16),
        ),
        in_specs=[smem] * 3 + [anywhere] * 5 + [vmem] * 3 + [anywhere],
        out_specs=(vmem, vmem, vmem),
        scratch_shapes=[
            pltpu.VMEM((requests, heads, rows, hd), bf16),
            pltpu.VMEM((requests, heads, rows, hd), bf16),
            pltpu.VMEM((requests, heads, G, nb, hd), bf16),
            pltpu.VMEM((depth, CH, feature, width), bf16),
            pltpu.VMEM((depth, B, requests, nb, feature), bf16),
            pltpu.VMEM((requests * heads, 2, nb, feature), bf16),
            pltpu.VMEM((B, CH, requests * nb, width), bf16),
            pltpu.VMEM((B, CH, requests * nb, width), bf16),
            pltpu.VMEM((CH, requests * nb, width), f32),
            pltpu.VMEM((requests, nb, rows), f32),
            pltpu.VMEM(out_weight.shape, bf16),
            pltpu.VMEM((requests, heads, resident_keys.shape[1], hd), bf16),
            pltpu.VMEM((requests, heads, resident_keys.shape[1], hd), bf16),
            pltpu.VMEM((n, share * pair, hd), bf16),
            pltpu.VMEM((n, pair, hd), f32),
            pltpu.VMEM((n, share * pair, hd), bf16),
            pltpu.VMEM((n, pair, hd), f32),
            pltpu.VMEM((n, share * pair, hd), bf16),
            pltpu.VMEM((2, pair, out_weight.shape[1]), f32),
            dma((CH + 4,)),
            dma((2, heads)),
            dma((2, heads)),
            dma((2, depth - 1, CH)),
            dma((2, depth - 1, CH)),
            dma((requests * heads, 2)),
            dma((2, requests, B)),
            dma((2, requests)),
            dma((2,)),
            dma((2,)),
            dma((B, CH)),
            dma((B, CH)),
            dma((n,)),
            dma((n,)),
            dma((n,)),
            dma((n,)),
            dma((n,)),
            dma((n,)),
            dma,
            dma,
        ],
        compiler_params=pltpu.CompilerParams(
            collective_id=0, has_side_effects=True, vmem_limit_bytes=60 * 1024 * 1024
        ),
    )(
        phase,
        ratio,
        resident_len,
        jnp.transpose(raw_keys, by_head),
        jnp.transpose(raw_values, by_head),
        jnp.transpose(beacon_queries, (0, 2, 3, 1, 4)),
        beacon_wk,
        beacon_wv,
        resident_keys,
        resident_values,
        jnp.transpose(decode_queries, (2, 3, 1, 0, 4)).reshape(heads, G * pair, hd),
        out_weight,
    )
    return (
        keys.reshape(requests, nb, heads, hd),
        values.reshape(requests, nb, heads, hd),
        jnp.transpose(projected.reshape(requests, steps, -1), (1, 0, 2)),
    )


def chosen_body(shard_count, head_count):
    def run(*arrays):
        requests, _, heads, hd = arrays[0].shape
        feature = arrays[6].shape[0]
        fits = (
            head_count == 2
            and shard_count == B * B
            and requests == 2
            and heads == B
            and 2 * feature == G * hd
        )
        return fused_body(shard_count, *arrays) if fits else body(*arrays)

    return run


def solution(mesh):
    return jax.shard_map(
        chosen_body(mesh.shape["seq"], mesh.shape["head"]),
        mesh=mesh,
        in_specs=(
            P(None, "seq", "head", None),
            P(None, "seq", "head", None),
            P(),
            P(),
            P(),
            P(None, "seq", "head", None, None),
            P("seq", "head"),
            P("seq", "head"),
            P(None, "seq", "head", None),
            P(None, "seq", "head", None),
            P(None, None, "head", None, None),
            P("head", "seq"),
        ),
        out_specs=(
            P(None, "seq", "head", None),
            P(None, "seq", "head", None),
            P(None, None, "seq"),
        ),
        check_vma=False,
    )
```
